128 devices in a mesh: wide: 8 (over z_hi, y), narrow: 16 (over z_lo, x, core).
Axes of the slice: x: 4, y: 4, z: 4 (z_hi: 2, z_lo: 2; z = z_hi * 2 + z_lo), core: 2. Of those that a mesh axis runs over, the one named last changes fastest.
Arguments:
- features: bfloat16 [262144, 128], P(('wide', 'narrow')), may hold values from -6 to 6
- band_tiles: int32 [2048, 16, 128, 128], P(('wide', 'narrow')), may hold values 0 or 1
- band_cols: int32 [2048, 16], P(('wide', 'narrow')), may hold values from 0 to 15
- off_tiles: int32 [128, 8, 128, 128], P(('wide', 'narrow')), may hold values 0 or 1
- req_block: int32 [128, 8], P(('wide', 'narrow')), may hold values from 0 to 15
- req_row: int32 [128, 8], P(('wide', 'narrow')), may hold values from 0 to 15
- req_valid: int32 [128, 8], P(('wide', 'narrow')), may hold values 0 or 1
- weight_self: bfloat16 [128, 256], replicated, may hold values from -0.5 to 0.5
- weight_neigh: bfloat16 [128, 256], replicated, may hold values from -1.5 to 1.5
- bias_term: bfloat16 [256], replicated, may hold values from -3 to 3
- cotangent: bfloat16 [262144, 256], P(('wide', 'narrow')), may hold values from -6 to 6
Outputs:
- layer_out: bfloat16 [262144, 256], P(('wide', 'narrow'))
- grad_features: float32 [262144, 128], P(('wide', 'narrow'))
- grad_self: float32 [128, 256], replicated
- grad_neigh: float32 [128, 256], replicated
- grad_bias: float32 [256], replicated
The draws below stay inside these ranges and needn't reach their ends.
All inputs are finite; a program needn't handle non-finite values. No bound on the sum of `band_tiles` or of `off_tiles` or of `req_valid` on one device may be relied on, other than what follows from the above.
Results may differ from the reference program's by a relative error of at most 0.007.
Values may be sent and summed in bfloat16 or wider, within the bound.
A program may use at most 128 MiB of HBM per device.

```python
import jax
import jax.numpy as jnp
from jax import lax

F_IN = 128
F_OUT = 256
BLOCK = 128
BLK_DEV = 16
NBLOCKS = 2048
NODES = 262144
N_WIDE = 8
N_NARROW = 16
DEVICES = 128


def set_ends(result, key, least, high):
    dims = result.shape
    place = [jax.random.randint(jax.random.fold_in(key, axis), (), 0, dims[axis]) for axis in range(len(dims))]
    result = result.at[tuple(place)].set(least)
    longest = dims.index(max(dims))
    place[longest] = (place[longest] + 1) % dims[longest]
    return result.at[tuple(place)].set(high)


def block_levels(stream_key, shape, shards, low, high):
    gain = 1.0
    for axis_at, parts in shards:
        steps = jax.random.uniform(jax.random.fold_in(jax.random.fold_in(stream_key, 6), axis_at), (parts,), jnp.float32, low / len(shards), high / len(shards))
        gain = gain * jnp.repeat(jnp.exp(steps), shape[axis_at] // parts).reshape((-1,) + (1,) * (len(shape) - 1 - axis_at))
    return gain


def scatter_about(rng, shape, scale, reach, split=(), kind=jnp.bfloat16):
    array = scale * jax.random.normal(rng, shape, jnp.float32)
    if split:
        array = array * block_levels(rng, shape, split, -0.22, 0.18)
    return jnp.clip(array, -reach, reach).astype(kind)


def setup_inputs(seed: int = 0) -> dict:
    arg_keys = jax.random.split(jax.random.key(seed), 12)
    return {
        "features": scatter_about(arg_keys[0], (NODES, F_IN), 1.0, 6.0, ((0, 128),)),
        "band_tiles": set_ends((jax.random.randint(arg_keys[1], (NBLOCKS, N_NARROW, BLOCK, BLOCK), 0, 64) < 1).astype(jnp.int32), jax.random.fold_in(arg_keys[1], 1), 0, 1),
        "band_cols": set_ends(jax.random.randint(arg_keys[2], (NBLOCKS, N_NARROW), 0, BLK_DEV), jax.random.fold_in(arg_keys[2], 1), 0, BLK_DEV - 1).astype(jnp.int32),
        "off_tiles": set_ends((jax.random.randint(arg_keys[3], (DEVICES, N_WIDE, BLOCK, BLOCK), 0, 8) < 1).astype(jnp.int32), jax.random.fold_in(arg_keys[3], 1), 0, 1),
        "req_block": set_ends(jax.random.randint(arg_keys[4], (DEVICES, N_WIDE), 0, BLK_DEV), jax.random.fold_in(arg_keys[4], 1), 0, BLK_DEV - 1).astype(jnp.int32),
        "req_row": set_ends(jax.random.randint(arg_keys[5], (DEVICES, N_WIDE), 0, BLK_DEV), jax.random.fold_in(arg_keys[5], 1), 0, BLK_DEV - 1).astype(jnp.int32),
        "req_valid": set_ends((jax.random.randint(arg_keys[6], (DEVICES, N_WIDE), 0, 4) < 3).astype(jnp.int32), jax.random.fold_in(arg_keys[6], 1), 0, 1),
        "weight_self": scatter_about(arg_keys[7], (F_IN, F_OUT), F_IN ** -0.5, 0.5),
        "weight_neigh": scatter_about(arg_keys[8], (F_IN, F_OUT), (F_IN // 8) ** -0.5, 1.5),
        "bias_term": scatter_about(arg_keys[9], (F_OUT,), 0.5, 3.0),
        "cotangent": scatter_about(arg_keys[10], (NODES, F_OUT), 1.0, 6.0, ((0, 128),)),
    }


def reference(features, band_tiles, band_cols, off_tiles, req_block, req_row, req_valid, weight_self, weight_neigh, bias_term, cotangent):
    feat_blocks = features.reshape(NBLOCKS, BLOCK, F_IN)
    block_ids = jnp.arange(NBLOCKS, dtype=jnp.int32)
    group_base = block_ids // BLK_DEV // N_NARROW * N_NARROW
    slab_ids = jnp.arange(N_NARROW, dtype=jnp.int32)

    def band_sum(totals, which):
        target = (group_base + which) * BLK_DEV + band_cols[:, which]
        tile = band_tiles[:, which].astype(jnp.float32)
        picked = feat_blocks[target].astype(jnp.float32)
        return (totals + jnp.einsum('gij,gjf->gif', tile, picked), None)
    gathered, _ = lax.scan(band_sum, jnp.zeros((NBLOCKS, BLOCK, F_IN), jnp.float32), slab_ids)
    degree = lax.optimization_barrier(jnp.sum(band_tiles.astype(jnp.float32), axis=(1, 3)))
    device_ids = jnp.arange(DEVICES, dtype=jnp.int32)[:, None]
    source = (jnp.arange(N_WIDE, dtype=jnp.int32)[None, :] * N_NARROW + device_ids % N_NARROW) * BLK_DEV + req_block
    target = device_ids * BLK_DEV + req_row
    masked = off_tiles.astype(jnp.float32) * req_valid.astype(jnp.float32)[:, :, None, None]
    pulled = jnp.einsum('dwij,dwjf->dwif', masked, feat_blocks[source].astype(jnp.float32))
    flat_target = target.reshape(-1)
    flat_source = source.reshape(-1)
    gathered = gathered.at[flat_target].add(pulled.reshape(-1, BLOCK, F_IN))
    degree = degree.at[flat_target].add(lax.optimization_barrier(jnp.sum(masked, axis=3)).reshape(-1, BLOCK))
    denom = degree + 1.0
    aggregate = (gathered / denom[:, :, None]).reshape(NODES, F_IN).astype(jnp.bfloat16)
    pre = jnp.dot(features, weight_self, preferred_element_type=jnp.float32)
    pre = pre + jnp.dot(aggregate, weight_neigh, preferred_element_type=jnp.float32) + bias_term.astype(jnp.float32)
    activated, pullback = jax.vjp(lambda value: jax.nn.gelu(value, approximate=True), pre)
    layer_out = activated.astype(jnp.bfloat16)
    grad_pre = pullback(cotangent.astype(jnp.float32))[0].astype(jnp.bfloat16)
    factor = NODES ** (-0.5)
    grad_self = jnp.dot(features.T, grad_pre, preferred_element_type=jnp.float32) * factor
    grad_neigh = jnp.dot(aggregate.T, grad_pre, preferred_element_type=jnp.float32) * factor
    grad_bias = lax.optimization_barrier(jnp.sum(grad_pre.astype(jnp.float32), axis=0)) * factor
    grad_agg = jnp.dot(grad_pre, weight_neigh.T, preferred_element_type=jnp.float32)
    signal = (grad_agg.reshape(NBLOCKS, BLOCK, F_IN) / denom[:, :, None]).astype(jnp.bfloat16)
    signal_wide = signal.astype(jnp.float32)
    local_ids = jnp.arange(BLK_DEV, dtype=jnp.int32)
    device_base = jnp.arange(DEVICES, dtype=jnp.int32) // N_NARROW * N_NARROW

    def band_back(totals, which):
        tile = band_tiles[:, which].astype(jnp.float32)
        moved = jnp.einsum('gji,gjf->gif', tile, signal_wide).reshape(DEVICES, BLK_DEV, BLOCK, F_IN)
        columns = band_cols[:, which].reshape(DEVICES, BLK_DEV)
        one_hot = (columns[:, :, None] == local_ids[None, None, :]).astype(jnp.float32)
        term = jnp.einsum('ebt,ebif->etif', one_hot, moved, precision=lax.Precision.HIGHEST)
        term = lax.optimization_barrier(term.astype(jnp.bfloat16)).astype(jnp.float32)
        dest = ((device_base + which)[:, None] * BLK_DEV + local_ids[None, :]).reshape(-1)
        return (totals.at[dest].add(term.reshape(-1, BLOCK, F_IN)), None)
    returned, _ = lax.scan(band_back, jnp.zeros((NBLOCKS, BLOCK, F_IN), jnp.float32), slab_ids)
    pushed = jnp.einsum('dwji,dwjf->dwif', masked, signal_wide[target])
    pushed = lax.optimization_barrier(pushed.astype(jnp.bfloat16)).astype(jnp.float32)
    returned = returned.at[flat_source].add(pushed.reshape(-1, BLOCK, F_IN))
    grad_features = jnp.dot(grad_pre, weight_self.T, preferred_element_type=jnp.float32) + returned.reshape(NODES, F_IN)
    return (layer_out, grad_features, grad_self, grad_neigh, grad_bias)
```

```python
import jax
import jax.numpy as jnp
from jax import lax
from jax.experimental import pallas as pl
from jax.experimental.pallas import tpu as pltpu
from jax.sharding import PartitionSpec as P

BF = jnp.bfloat16
F32 = jnp.float32
I32 = jnp.int32
MESH = pl.DeviceIdType.MESH
NT = (((1,), (1,)), ((), ()))
TN = (((0,), (0,)), ((), ()))

OFF = ((0, 0), (1, 0), (3, 0), (0, 1), (2, 0), (1, 1), (3, 1), (2, 1))
SEND = ((2, 1), (1, 1), (3, 1), (1, 0), (3, 0), (2, 0), (0, 1), (0, 0))
WIDE = 8
GELU_A = 0.7978845608
GELU_B = 0.044715

S_OWN, S_RELAY, S_PAIR, S_REQ, S_FET, S_PUSH = 0, 8, 16, 32, 40, 48
S_GPAIR, S_GW, S_GN, S_GA, S_GB, S_PART, S_RS, S_COUNT = 56, 57, 65, 73, 81, 82, 90, 104
L_TILE, L_FEAT, L_OFF, L_COT, L_IDX, L_LO, L_GF, L_G, L_COUNT = 0, 3, 4, 5, 6, 7, 8, 24, 25


def dot(a, b, dims=None):
    if dims is None:
        return jnp.dot(a, b, preferred_element_type=F32)
    return lax.dot_general(a, b, dims, preferred_element_type=F32)


def body(
    feat, tiles, cols, cols_v, offs, rblock, rrow, rvalid, w_self, w_neigh, bias, cot,
    lo_out, gf_out, g_out,
    f0, f1, f2, f3, f4, f5, f6, f7,
    tileb, stage, offi, offb, cotv, acc, degs, fa, gp, lo, sigt, runs, wcat,
    sd2d, rd2d, pbuf, rz, rxp, rxm, rha, rhb, rfp, rfm, rfz, baset, gfv,
    idx_v, idx, reqs, reqr, sel, fetr, pull, pushs, pushr,
    gsrc, grx, gsum, gwr, gown, gnr, gfin, gall,
    ss, rs, ls,
):
    fs = (f0, f1, f2, f3, f4, f5, f6, f7)
    me = lax.axis_index("narrow")
    w = lax.axis_index("wide")
    core = me % 2
    chip = me // 2
    x = chip % 4
    z = chip // 4

    def chip_at(dx, dz):
        return ((z + dz) % 2) * 4 + (x + dx) % 4

    def near(dx, dz):
        return (w, chip_at(dx, dz) * 2 + core)

    partner = (w, chip * 2 + (1 - core))
    xp, xm, zz = near(1, 0), near(3, 0), near(0, 1)

    def far(j):
        return ((w + j) % WIDE, me)

    pending = []

    def remote(src, dst, i, dev):
        return pltpu.make_async_remote_copy(
            src_ref=src, dst_ref=dst, send_sem=ss.at[i], recv_sem=rs.at[i],
            device_id=dev, device_id_type=MESH,
        )

    def send(src, dst, i, dev):
        c = remote(src, dst, i, dev)
        c.start()
        pending.append(c)
        return c

    def load_tiles(b, slot):
        return pltpu.make_async_copy(tiles.at[b], stage.at[slot], ls.at[L_TILE + slot])

    own = pltpu.make_async_copy(feat, f0.at[core], ls.at[L_FEAT])
    own.start()
    off_load = pltpu.make_async_copy(offs, offi, ls.at[L_OFF])
    off_load.start()
    load_tiles(0, 0).start()
    load_tiles(1, 1).start()
    cot_load = pltpu.make_async_copy(cot, cotv, ls.at[L_COT])
    cot_load.start()

    bar = pltpu.get_barrier_semaphore()
    pl.semaphore_signal(bar, inc=1, device_id=partner, device_id_type=MESH)
    for dx, dz in OFF[1:]:
        pl.semaphore_signal(bar, inc=1, device_id=near(dx, dz), device_id_type=MESH)
    for j in range(1, WIDE):
        pl.semaphore_signal(bar, inc=1, device_id=far(j), device_id_type=MESH)
    for b in range(WIDE):
        reqs[b] = jnp.full((8, 128), rblock[0, b], I32)
    pl.semaphore_wait(bar, 15)

    lo_h, hi_h = pl.ds(0, 8), pl.ds(8, 8)
    halves = (lo_h, hi_h)
    to_p = [None, None]
    to_m = [None, None]
    to_z = [None, None]
    to_p[0] = send(feat.at[lo_h], f2.at[core, lo_h], S_OWN + 0, xp)
    to_m[1] = send(feat.at[hi_h], f1.at[core, hi_h], S_OWN + 1, xm)
    to_z[0] = send(feat.at[lo_h], f3.at[core, lo_h], S_OWN + 2, zz)
    req_c = [None] * WIDE
    for j in range(1, WIDE):
        req_c[j] = send(reqs.at[(w + j) % WIDE], reqr.at[WIDE - j], S_REQ + j, far(j))
    to_p[1] = send(feat.at[hi_h], f2.at[core, hi_h], S_OWN + 3, xp)
    to_m[0] = send(feat.at[lo_h], f1.at[core, lo_h], S_OWN + 4, xm)
    to_z[1] = send(feat.at[hi_h], f3.at[core, hi_h], S_OWN + 5, zz)
    pair0 = send(feat, f0.at[core], S_PAIR, partner)

    c16 = cols_v[...]
    ib = lax.broadcasted_iota(I32, (16, 16), 0)
    rank = jnp.zeros((16, 16), I32)
    prev = jnp.zeros((16, 16), I32)
    count = jnp.zeros((16, 16), I32)
    upto = jnp.zeros((16, 16), I32)
    for b in range(16):
        row = jnp.broadcast_to(c16[b : b + 1, :], (16, 16))
        same = row == c16
        before = same & (ib > b)
        rank += jnp.where((row < c16) | before, 1, 0)
        prev += jnp.where(before, 1, 0)
        count += jnp.where(row == ib, 1, 0)
        upto += jnp.where(row <= ib, 1, 0)
    order = jnp.zeros((16, 16), I32)
    keep = jnp.zeros((16, 16), I32)
    for b in range(16):
        hit = jnp.broadcast_to(rank[b : b + 1, :], (16, 16)) == ib
        order += jnp.where(hit, b, 0)
        keep += jnp.where(hit & (jnp.broadcast_to(prev[b : b + 1, :], (16, 16)) > 0), 1, 0)
    idx_v[...] = jnp.zeros((64, 128), I32)
    idx_v[0:16, 0:16] = order
    idx_v[16:32, 0:16] = keep
    idx_v[32:48, 0:16] = jnp.maximum(upto - 1, 0)
    idx_v[48:64, 0:16] = jnp.where(count > 0, 1, 0)
    idx_load = pltpu.make_async_copy(idx_v, idx, ls.at[L_IDX])
    idx_load.start()
    wcat[0:128, :] = w_self[...]
    wcat[128:256, :] = w_neigh[...]

    own.wait()
    off_load.wait()
    reqr[0] = reqs[w]
    for j in range(WIDE):
        offb[j] = (offi[j] * rvalid[0, j]).astype(BF)
    fet_c = [None] * WIDE
    for j in range(1, WIDE):
        req_c[j].wait_recv()
    for j in range(1, WIDE):
        asked = reqr[WIDE - j][0:1, :]

        def pick(t, total, asked=asked):
            m = jnp.where(asked == t, 1.0, 0.0)
            return total + f0[core, t].astype(F32) * m

        sel[j] = lax.fori_loop(0, 16, pick, jnp.zeros((128, 128), F32)).astype(BF)
        fet_c[j] = send(sel.at[j], fetr.at[j], S_FET + j, far(WIDE - j))

    def convert(b, carry):
        slot = b % 3
        load_tiles(b, slot).wait()

        @pl.when(b + 2 < 16)
        def _():
            load_tiles(b + 2, (b + 2) % 3).start()

        total = jnp.zeros((128, 128), I32)
        for c in range(8):
            lft = stage[slot, 2 * c]
            rgt = stage[slot, 2 * c + 1]
            total += lft + rgt
            tileb[b, c] = jnp.concatenate([lft, rgt], axis=1).astype(F32).astype(BF)
        for j in range(WIDE):
            use = jnp.where(rrow[0, j] == b, rvalid[0, j], 0)
            total += offi[j] * use
        degs[b] = total.astype(F32).astype(BF)
        return carry

    lax.fori_loop(0, 16, convert, 0)

    def band(b, o):
        c = chip_at(*OFF[o])
        rhs = jnp.concatenate(
            [fs[o][0, cols[b, 2 * c]], fs[o][1, cols[b, 2 * c + 1]]], axis=0
        )
        return dot(tileb[b, c], rhs)

    def across(o, h):
        return send(fs[o].at[core, halves[h]], fs[o].at[core, halves[h]], S_PAIR + 2 * o + h, partner)

    swap = [[None, None] for _ in OFF]
    to_p[0].wait_recv()
    rel_p = send(f2.at[core, lo_h], f4.at[core, lo_h], S_RELAY + 0, xp)
    to_m[1].wait_recv()
    rel_m = send(f1.at[core, hi_h], f4.at[core, hi_h], S_RELAY + 1, xm)
    swap[2][0] = across(2, 0)
    swap[1][1] = across(1, 1)
    to_z[0].wait_recv()
    z_p = [None, None]
    z_m = [None, None]
    z_p[0] = send(f3.at[core, lo_h], f6.at[core, lo_h], S_RELAY + 2, xp)
    z_m[0] = send(f3.at[core, lo_h], f5.at[core, lo_h], S_RELAY + 3, xm)
    swap[3][0] = across(3, 0)

    pair0.wait_recv()

    def first(b, carry):
        acc[b] = band(b, 0)
        return carry

    lax.fori_loop(0, 16, first, 0, unroll=2)

    to_z[1].wait_recv()
    z_p[1] = send(f3.at[core, hi_h], f6.at[core, hi_h], S_RELAY + 4, xp)
    z_m[1] = send(f3.at[core, hi_h], f5.at[core, hi_h], S_RELAY + 5, xm)
    swap[3][1] = across(3, 1)
    to_p[1].wait_recv()
    swap[2][1] = across(2, 1)
    to_m[0].wait_recv()
    swap[1][0] = across(1, 0)

    for j in range(1, WIDE):
        fet_c[j].wait_recv()
    fetr[0] = f0[core, rblock[0, w]]
    for j in range(WIDE):
        pull[j] = dot(offb[(w + j) % WIDE], fetr[j])

    for o in (1, 2, 3):
        swap[o][0].wait_recv()
        swap[o][1].wait_recv()

    def second(b, carry):
        total = acc[b] + band(b, 1) + band(b, 2) + band(b, 3)
        for j in range(WIDE):
            use = jnp.where(rrow[0, (w + j) % WIDE] == b, 1, 0).astype(F32)
            total += pull[j] * use
        acc[b] = total
        return carry

    lax.fori_loop(0, 16, second, 0, unroll=2)

    rel_p.wait_recv()
    zr = [None, None]
    zr[0] = send(f4.at[core, lo_h], f7.at[core, lo_h], S_RELAY + 6, zz)
    swap[4][0] = across(4, 0)
    rel_m.wait_recv()
    zr[1] = send(f4.at[core, hi_h], f7.at[core, hi_h], S_RELAY + 7, zz)
    swap[4][1] = across(4, 1)
    swap[4][0].wait_recv()
    swap[4][1].wait_recv()

    def third(b, carry):
        acc[b] += band(b, 4)
        return carry

    lax.fori_loop(0, 16, third, 0, unroll=2)
    idx_load.wait()
    cot_load.wait()

    for h in range(2):
        z_p[h].wait_recv()
        swap[6][h] = across(6, h)
        z_m[h].wait_recv()
        swap[5][h] = across(5, h)
        zr[h].wait_recv()
        swap[7][h] = across(7, h)
    for o in (5, 6, 7):
        swap[o][0].wait_recv()
        swap[o][1].wait_recv()

    ones = jnp.ones((128, 128), BF)

    def dense(b, carry):
        total = acc[b] + band(b, 5) + band(b, 6) + band(b, 7)
        deg = degs[b]
        agg = (total / (dot(deg, ones) + 1.0)).astype(BF)
        both = jnp.concatenate([f0[core, b], agg], axis=1)
        fa[b] = both
        v = dot(both, wcat[...]) + bias[...].astype(F32)
        v2 = v * v
        th = jnp.tanh(GELU_A * (v + GELU_B * v * v2))
        up = 0.5 * (1.0 + th)
        lo[b] = (v * up).astype(BF)
        slope = up + 0.5 * v * (1.0 - th * th) * (GELU_A + (3.0 * GELU_A * GELU_B) * v2)
        g = (cotv[b].astype(F32) * slope).astype(BF)
        gp[b] = g
        back = dot(w_neigh[...], g, NT)
        sigt[b] = (back / (dot(ones, deg, NT) + 1.0)).astype(BF)
        return carry

    lax.fori_loop(0, 16, dense, 0, unroll=2)
    lo_c = pltpu.make_async_copy(lo, lo_out, ls.at[L_LO])
    lo_c.start()

    def product(n2, k):
        b = idx[k, n2]
        lanes = pl.ds(pl.multiple_of((n2 % 2) * 128, 128), 128)
        return dot(sigt[b], tileb[b, n2 // 2, :, lanes])

    def part(n2):
        total = product(n2, 0)
        runs[0] = total
        for k in range(1, 16):
            total = total * idx[16 + k, n2].astype(F32) + product(n2, k)
            runs[k] = total

    def run_of(n2, t):
        return runs[idx[32 + t, n2]] * idx[48 + t, n2].astype(F32)

    def chip_of(j):
        dx, dz = 0, 0
        for i, (ax, az) in enumerate(SEND):
            dx = dx + jnp.where(j == i, ax, 0)
            dz = dz + jnp.where(j == i, az, 0)
        return chip_at(dx, dz)

    def swap_part(j):
        return remote(sd2d.at[j], rd2d.at[j], S_PART + j, partner)

    def link(i, src, dst, dev):
        return remote(src, dst, S_RS + i, dev)

    leaf = [
        link(0, pbuf.at[0], rz, zz),
        link(1, pbuf.at[1], rxm, xp),
        link(2, pbuf.at[2], rxp, xm),
        link(3, pbuf.at[3, hi_h], rfm.at[hi_h], xp),
        link(4, pbuf.at[4, lo_h], rfp.at[lo_h], xm),
    ]

    def step(j, carry):
        @pl.when(j < 8)
        def _():
            n2 = chip_of(j) * 2 + (1 - core)
            part(n2)
            for t in range(16):
                sd2d[j, t] = run_of(n2, t).astype(BF)
            swap_part(j).start()

        @pl.when(j > 0)
        def _():
            i = j - 1
            n2 = chip_of(i) * 2 + core
            part(n2)
            swap_part(i).wait_recv()
            for t in range(16):
                pbuf[i, t] = (run_of(n2, t) + rd2d[i, t].astype(F32)).astype(BF)
            for q in range(5):

                @pl.when(i == q)
                def _(q=q):
                    leaf[q].start()

        return carry

    lax.fori_loop(0, 9, step, 0)
    pending.extend(leaf)

    push_c = [None] * WIDE
    for j in range(WIDE):
        there = (w + j) % WIDE
        sums = dot(sigt[rrow[0, there]], offb[there]).astype(BF)
        if j:
            pushs[j] = sums
            push_c[j] = send(pushs.at[j], pushr.at[WIDE - j], S_PUSH + j, far(j))
        else:
            pushr[0] = sums

    gsum_w = jnp.zeros((256, 256), F32)

    def weights(b, tot):
        return tot + dot(fa[b], gp[b], TN)

    def biases(b, tot):
        return tot + dot(jnp.ones((8, 128), BF), gp[b])

    grad_w = lax.fori_loop(0, 16, weights, gsum_w)
    grad_b = lax.fori_loop(0, 16, biases, jnp.zeros((8, 256), F32))
    for h in range(2):
        for p in range(8):
            gsrc[h, p, 0:16] = grad_w[h * 128 + p * 16 : h * 128 + p * 16 + 16]
            gsrc[h, p, 16:24] = grad_b
    g_pair = send(gsrc.at[1 - core], grx, S_GPAIR, partner)

    def base(b, carry):
        baset[b] = dot(w_self[...], gp[b], NT)
        return carry

    lax.fori_loop(0, 16, base, 0, unroll=2)

    g_pair.wait_recv()
    gsum[...] = gsrc[core] + grx[...]
    gw_c = [None] * WIDE
    for j in range(1, WIDE):
        gw_c[j] = send(gsum.at[(w + j) % WIDE], gwr.at[WIDE - j], S_GW + j, far(j))

    leaf[0].wait_recv()

    def add_one(t, carry):
        pbuf[5, t] = (pbuf[5, t].astype(F32) + rz[t].astype(F32)).astype(BF)
        return carry

    lax.fori_loop(0, 16, add_one, 0)
    half_a = send(pbuf.at[5, lo_h], rha, S_RS + 5, xp)
    half_b = send(pbuf.at[5, hi_h], rhb, S_RS + 6, xm)

    leaf[1].wait_recv()
    leaf[2].wait_recv()

    def add_two(t, carry):
        both = rxp[t].astype(F32) + rxm[t].astype(F32)
        pbuf[6, t] = (pbuf[6, t].astype(F32) + both).astype(BF)
        return carry

    lax.fori_loop(0, 16, add_two, 0)
    last_z = send(pbuf.at[6], rfz, S_RS + 7, zz)

    for j in range(1, WIDE):
        gw_c[j].wait_recv()
    tot = gsum[w]
    for j in range(1, WIDE):
        tot += gwr[j]
    gown[...] = tot
    gn_c = [None] * WIDE
    for o in range(1, 8):
        gn_c[o] = send(gown, gnr.at[chip], S_GN + o, near(*OFF[o]))

    for j in range(1, WIDE):
        push_c[j].wait_recv()

    def off_back(t, carry):
        total = baset[t] + pbuf[7, t].astype(F32)
        for j in range(WIDE):
            m = jnp.where(reqr[j][0:1, :] == t, 1.0, 0.0)
            total += pushr[j].astype(F32) * m
        baset[t] = total
        return carry

    lax.fori_loop(0, 16, off_back, 0)

    for o in range(1, 8):
        gn_c[o].wait_recv()
    gnr[chip] = gown[...]
    tot = gnr[0]
    for c in range(1, 8):
        tot += gnr[c]
    gfin[w] = tot
    ga_c = [None] * WIDE
    for j in range(1, WIDE):
        ga_c[j] = send(gfin.at[w], gfin.at[w], S_GA + j, far(j))

    half_a.wait_recv()

    def add_a(t, carry):
        pbuf[3, t] = (pbuf[3, t].astype(F32) + rha[t].astype(F32)).astype(BF)
        return carry

    lax.fori_loop(0, 8, add_a, 0)
    last_p = send(pbuf.at[3, lo_h], rfm.at[lo_h], S_RS + 8, xp)
    half_b.wait_recv()

    def add_b(t, carry):
        pbuf[4, 8 + t] = (pbuf[4, 8 + t].astype(F32) + rhb[t].astype(F32)).astype(BF)
        return carry

    lax.fori_loop(0, 8, add_b, 0)
    last_m = send(pbuf.at[4, hi_h], rfp.at[hi_h], S_RS + 9, xm)

    for j in range(1, WIDE):
        ga_c[j].wait_recv()
    gall[core] = gfin[...]
    g_last = send(gfin, gall.at[core], S_GB, partner)

    leaf[3].wait_recv()
    leaf[4].wait_recv()
    last_z.wait_recv()
    g_last.wait_recv()
    g_c = pltpu.make_async_copy(gall, g_out, ls.at[L_G])
    g_c.start()

    gf_c = []

    def finish(h):
        for i in range(8):
            t = 8 * h + i
            total = baset[t] + rfp[t].astype(F32) + rfm[t].astype(F32) + rfz[t].astype(F32)
            gfv[t] = total.T
            c = pltpu.make_async_copy(gfv.at[t], gf_out.at[t], ls.at[L_GF + t])
            c.start()
            gf_c.append(c)

    last_p.wait_recv()
    finish(0)
    last_m.wait_recv()
    finish(1)

    for c in gf_c:
        c.wait()
    lo_c.wait()
    g_c.wait()
    for c in pending:
        c.wait_send()

    def drain(j, carry):
        swap_part(j).wait_send()
        return carry

    lax.fori_loop(0, 8, drain, 0)


def shards(
    features, band_tiles, band_cols, off_tiles, req_block, req_row, req_valid,
    weight_self, weight_neigh, bias_term, cotangent,
):
    hbm = pl.BlockSpec(memory_space=pl.ANY)
    vmem = pl.BlockSpec(memory_space=pltpu.VMEM)
    smem = pl.BlockSpec(memory_space=pltpu.SMEM)
    block = (16, 128, 128)
    v = pltpu.VMEM
    scratch = [v((2,) + block, BF) for _ in range(8)]
    scratch += [
        v((16, 8, 128, 256), BF),
        v((3,) + block, I32),
        v((8, 128, 128), I32),
        v((8, 128, 128), BF),
        v((16, 128, 256), BF),
        v(block, F32),
        v(block, BF),
        v((16, 128, 256), BF),
        v((16, 128, 256), BF),
        v((16, 128, 256), BF),
        v(block, BF),
        v(block, F32),
        v((256, 256), BF),
        v((8,) + block, BF),
        v((8,) + block, BF),
        v((8,) + block, BF),
        v(block, BF),
        v(block, BF),
        v(block, BF),
        v((8, 128, 128), BF),
        v((8, 128, 128), BF),
        v(block, BF),
        v(block, BF),
        v(block, BF),
        v(block, F32),
        v(block, F32),
        v((64, 128), I32),
        pltpu.SMEM((64, 128), I32),
        v((8, 8, 128), I32),
        v((8, 8, 128), I32),
        v((8, 128, 128), BF),
        v((8, 128, 128), BF),
        v((8, 128, 128), F32),
        v((8, 128, 128), BF),
        v((8, 128, 128), BF),
        v((2, 8, 24, 256), F32),
        v((8, 24, 256), F32),
        v((8, 24, 256), F32),
        v((8, 24, 256), F32),
        v((24, 256), F32),
        v((8, 24, 256), F32),
        v((8, 24, 256), F32),
        v((2, 8, 24, 256), F32),
        pltpu.SemaphoreType.DMA((S_COUNT,)),
        pltpu.SemaphoreType.DMA((S_COUNT,)),
        pltpu.SemaphoreType.DMA((L_COUNT,)),
    ]
    layer_out, grad_feat, grads = pl.pallas_call(
        body,
        out_shape=(
            jax.ShapeDtypeStruct((16, 128, 256), BF),
            jax.ShapeDtypeStruct(block, F32),
            jax.ShapeDtypeStruct((2, 8, 24, 256), F32),
        ),
        in_specs=[hbm, hbm, smem, vmem, hbm, smem, smem, smem, vmem, vmem, vmem, hbm],
        out_specs=(hbm, hbm, hbm),
        scratch_shapes=scratch,
        compiler_params=pltpu.CompilerParams(
            collective_id=0, has_side_effects=True, vmem_limit_bytes=60 * 1024 * 1024
        ),
        name="sage",
    )(
        features.reshape(block), band_tiles, band_cols, band_cols, off_tiles[0],
        req_block, req_row, req_valid, weight_self, weight_neigh,
        bias_term.reshape(1, 256), cotangent.reshape(16, 128, 256),
    )
    factor = 262144 ** (-0.5)
    grad_self = grads[0, :, 0:16].reshape(128, 256) * factor
    grad_neigh = grads[1, :, 0:16].reshape(128, 256) * factor
    grad_bias = grads[0, 0, 16] * factor
    return (
        layer_out.reshape(2048, 256),
        grad_feat.reshape(2048, 128),
        grad_self,
        grad_neigh,
        grad_bias,
    )


def solution(mesh):
    placed = (
        P(("wide", "narrow"), None),
        P(("wide", "narrow"), None, None, None),
        P(("wide", "narrow"), None),
        P(("wide", "narrow"), None, None, None),
        P(("wide", "narrow"), None),
        P(("wide", "narrow"), None),
        P(("wide", "narrow"), None),
        P(),
        P(),
        P(),
        P(("wide", "narrow"), None),
    )
    return jax.shard_map(
        shards,
        mesh=mesh,
        in_specs=placed,
        out_specs=(P(("wide", "narrow"), None), P(("wide", "narrow"), None), P(), P(), P()),
        check_vma=False,
    )
```

```python
import jax
import jax.numpy as jnp
from jax import lax
from jax.experimental import pallas as pl
from jax.experimental.pallas import tpu as pltpu
from jax.sharding import PartitionSpec as P

BF = jnp.bfloat16
F32 = jnp.float32
I32 = jnp.int32
MESH = pl.DeviceIdType.MESH
NT = (((1,), (1,)), ((), ()))
TN = (((0,), (0,)), ((), ()))

OFF = ((0, 0), (1, 0), (3, 0), (0, 1), (2, 0), (1, 1), (3, 1), (2, 1))
SEND = ((2, 1), (1, 1), (3, 1), (1, 0), (3, 0), (2, 0), (0, 1), (0, 0))
WIDE = 8
GELU_A = 0.7978845608
GELU_B = 0.044715

S_OWN, S_RELAY, S_PAIR, S_REQ, S_FET, S_PUSH = 0, 8, 16, 32, 40, 48
S_GPAIR, S_GW, S_GN, S_GA, S_GB, S_PART, S_RS, S_COUNT = 56, 57, 65, 73, 81, 82, 90, 104
L_TILE, L_FEAT, L_OFF, L_COT, L_IDX, L_LO, L_GF, L_G, L_COUNT = 0, 3, 4, 5, 6, 7, 8, 24, 25


def dot(a, b, dims=None):
    if dims is None:
        return jnp.dot(a, b, preferred_element_type=F32)
    return lax.dot_general(a, b, dims, preferred_element_type=F32)


def body(
    feat, tiles, cols, cols_v, offs, rblock, rrow, rvalid, w_self, w_neigh, bias, cot,
    lo_out, gf_out, g_out,
    f0, f1, f2, f3, f4, f5, f6, f7,
    tileb, stage, offi, offb, cotv, acc, degs, fa, gp, lo, sigt, runs, wcat,
    sd2d, rd2d, pbuf, rz, rxp, rxm, rha, rhb, rfp, rfm, rfz, baset, gfv,
    idx_v, idx, reqs, reqr, sel, fetr, pull, pushs, pushr,
    gsrc, grx, gsum, gwr, gown, gnr, gfin, gall,
    ss, rs, ls,
):
    fs = (f0, f1, f2, f3, f4, f5, f6, f7)
    me = lax.axis_index("narrow")
    w = lax.axis_index("wide")
    core = me % 2
    chip = me // 2
    x = chip % 4
    z = chip // 4

    def chip_at(dx, dz):
        return ((z + dz) % 2) * 4 + (x + dx) % 4

    def near(dx, dz):
        return (w, chip_at(dx, dz) * 2 + core)

    partner = (w, chip * 2 + (1 - core))
    xp, xm, zz = near(1, 0), near(3, 0), near(0, 1)

    def far(j):
        return ((w + j) % WIDE, me)

    pending = []

    def remote(src, dst, i, dev):
        return pltpu.make_async_remote_copy(
            src_ref=src, dst_ref=dst, send_sem=ss.at[i], recv_sem=rs.at[i],
            device_id=dev, device_id_type=MESH,
        )

    def send(src, dst, i, dev):
        c = remote(src, dst, i, dev)
        c.start()
        pending.append(c)
        return c

    def load_tiles(b, slot):
        return pltpu.make_async_copy(tiles.at[b], stage.at[slot], ls.at[L_TILE + slot])

    own = pltpu.make_async_copy(feat, f0.at[core], ls.at[L_FEAT])
    own.start()
    off_load = pltpu.make_async_copy(offs, offi, ls.at[L_OFF])
    off_load.start()
    load_tiles(0, 0).start()
    load_tiles(1, 1).start()
    cot_load = pltpu.make_async_copy(cot, cotv, ls.at[L_COT])
    cot_load.start()

    bar = pltpu.get_barrier_semaphore()
    pl.semaphore_signal(bar, inc=1, device_id=partner, device_id_type=MESH)
    for dx, dz in OFF[1:]:
        pl.semaphore_signal(bar, inc=1, device_id=near(dx, dz), device_id_type=MESH)
    for j in range(1, WIDE):
        pl.semaphore_signal(bar, inc=1, device_id=far(j), device_id_type=MESH)
    for b in range(WIDE):
        reqs[b] = jnp.full((8, 128), rblock[0, b], I32)
    pl.semaphore_wait(bar, 15)

    lo_h, hi_h = pl.ds(0, 8), pl.ds(8, 8)
    halves = (lo_h, hi_h)
    to_p = [None, None]
    to_m = [None, None]
    to_z = [None, None]
    req_c = [None] * WIDE
    for j in range(1, WIDE):
        req_c[j] = send(reqs.at[(w + j) % WIDE], reqr.at[WIDE - j], S_REQ + j, far(j))
    to_p[0] = send(feat.at[lo_h], f2.at[core, lo_h], S_OWN + 0, xp)
    to_m[1] = send(feat.at[hi_h], f1.at[core, hi_h], S_OWN + 1, xm)
    to_z[0] = send(feat.at[lo_h], f3.at[core, lo_h], S_OWN + 2, zz)
    to_p[1] = send(feat.at[hi_h], f2.at[core, hi_h], S_OWN + 3, xp)
    to_m[0] = send(feat.at[lo_h], f1.at[core, lo_h], S_OWN + 4, xm)
    to_z[1] = send(feat.at[hi_h], f3.at[core, hi_h], S_OWN + 5, zz)
    pair0 = send(feat, f0.at[core], S_PAIR, partner)

    c16 = cols_v[...]
    ib = lax.broadcasted_iota(I32, (16, 16), 0)
    rank = jnp.zeros((16, 16), I32)
    prev = jnp.zeros((16, 16), I32)
    count = jnp.zeros((16, 16), I32)
    upto = jnp.zeros((16, 16), I32)
    for b in range(16):
        row = jnp.broadcast_to(c16[b : b + 1, :], (16, 16))
        same = row == c16
        before = same & (ib > b)
        rank += jnp.where((row < c16) | before, 1, 0)
        prev += jnp.where(before, 1, 0)
        count += jnp.where(row == ib, 1, 0)
        upto += jnp.where(row <= ib, 1, 0)
    order = jnp.zeros((16, 16), I32)
    keep = jnp.zeros((16, 16), I32)
    for b in range(16):
        hit = jnp.broadcast_to(rank[b : b + 1, :], (16, 16)) == ib
        order += jnp.where(hit, b, 0)
        keep += jnp.where(hit & (jnp.broadcast_to(prev[b : b + 1, :], (16, 16)) > 0), 1, 0)
    idx_v[...] = jnp.zeros((64, 128), I32)
    idx_v[0:16, 0:16] = order
    idx_v[16:32, 0:16] = keep
    idx_v[32:48, 0:16] = jnp.maximum(upto - 1, 0)
    idx_v[48:64, 0:16] = jnp.where(count > 0, 1, 0)
    idx_load = pltpu.make_async_copy(idx_v, idx, ls.at[L_IDX])
    idx_load.start()
    wcat[0:128, :] = w_self[...]
    wcat[128:256, :] = w_neigh[...]

    own.wait()
    off_load.wait()

    def convert(b, carry):
        slot = b % 3
        load_tiles(b, slot).wait()

        @pl.when(b + 2 < 16)
        def _():
            load_tiles(b + 2, (b + 2) % 3).start()

        total = jnp.zeros((128, 128), I32)
        for c in range(8):
            lft = stage[slot, 2 * c]
            rgt = stage[slot, 2 * c + 1]
            total += lft + rgt
            tileb[b, c] = jnp.concatenate([lft, rgt], axis=1).astype(F32).astype(BF)
        for j in range(WIDE):
            use = jnp.where(rrow[0, j] == b, rvalid[0, j], 0)
            total += offi[j] * use
        degs[b] = total.astype(F32).astype(BF)
        return carry

    lax.fori_loop(0, 6, convert, 0)

    reqr[0] = reqs[w]
    for j in range(WIDE):
        offb[j] = (offi[j] * rvalid[0, j]).astype(BF)
    fet_c = [None] * WIDE
    for j in range(1, WIDE):
        req_c[j].wait_recv()
    for j in range(1, WIDE):
        asked = reqr[WIDE - j][0:1, :]

        def pick(t, total, asked=asked):
            m = jnp.where(asked == t, 1.0, 0.0)
            return total + f0[core, t].astype(F32) * m

        sel[j] = lax.fori_loop(0, 16, pick, jnp.zeros((128, 128), F32)).astype(BF)
        fet_c[j] = send(sel.at[j], fetr.at[j], S_FET + j, far(WIDE - j))

    def band(b, o):
        c = chip_at(*OFF[o])
        rhs = jnp.concatenate(
            [fs[o][0, cols[b, 2 * c]], fs[o][1, cols[b, 2 * c + 1]]], axis=0
        )
        return dot(tileb[b, c], rhs)

    def across(o, h):
        return send(fs[o].at[core, halves[h]], fs[o].at[core, halves[h]], S_PAIR + 2 * o + h, partner)

    swap = [[None, None] for _ in OFF]
    to_p[0].wait_recv()
    rel_p = send(f2.at[core, lo_h], f4.at[core, lo_h], S_RELAY + 0, xp)
    to_m[1].wait_recv()
    rel_m = send(f1.at[core, hi_h], f4.at[core, hi_h], S_RELAY + 1, xm)
    swap[2][0] = across(2, 0)
    swap[1][1] = across(1, 1)
    to_z[0].wait_recv()
    z_p = [None, None]
    z_m = [None, None]
    z_p[0] = send(f3.at[core, lo_h], f6.at[core, lo_h], S_RELAY + 2, xp)
    z_m[0] = send(f3.at[core, lo_h], f5.at[core, lo_h], S_RELAY + 3, xm)
    swap[3][0] = across(3, 0)

    lax.fori_loop(6, 16, convert, 0)
    pair0.wait_recv()

    def first(b, carry):
        acc[b] = band(b, 0)
        return carry

    lax.fori_loop(0, 16, first, 0, unroll=2)

    to_z[1].wait_recv()
    z_p[1] = send(f3.at[core, hi_h], f6.at[core, hi_h], S_RELAY + 4, xp)
    z_m[1] = send(f3.at[core, hi_h], f5.at[core, hi_h], S_RELAY + 5, xm)
    swap[3][1] = across(3, 1)
    to_p[1].wait_recv()
    swap[2][1] = across(2, 1)
    to_m[0].wait_recv()
    swap[1][0] = across(1, 0)

    for o in (1, 2, 3):
        swap[o][0].wait_recv()
        swap[o][1].wait_recv()

    def second(b, carry):
        total = acc[b] + band(b, 1) + band(b, 2) + band(b, 3)
        acc[b] = total
        return carry

    lax.fori_loop(0, 16, second, 0, unroll=2)

    rel_p.wait_recv()
    zr = [None, None]
    zr[0] = send(f4.at[core, lo_h], f7.at[core, lo_h], S_RELAY + 6, zz)
    swap[4][0] = across(4, 0)
    rel_m.wait_recv()
    zr[1] = send(f4.at[core, hi_h], f7.at[core, hi_h], S_RELAY + 7, zz)
    swap[4][1] = across(4, 1)
    for j in range(1, WIDE):
        fet_c[j].wait_recv()
    fetr[0] = f0[core, rblock[0, w]]
    for j in range(WIDE):
        pull[j] = dot(offb[(w + j) % WIDE], fetr[j])

    swap[4][0].wait_recv()
    swap[4][1].wait_recv()

    def third(b, carry):
        total = acc[b] + band(b, 4)
        for j in range(WIDE):
            use = jnp.where(rrow[0, (w + j) % WIDE] == b, 1, 0).astype(F32)
            total += pull[j] * use
        acc[b] = total
        return carry

    lax.fori_loop(0, 16, third, 0, unroll=2)
    idx_load.wait()
    cot_load.wait()

    for h in range(2):
        z_p[h].wait_recv()
        swap[6][h] = across(6, h)
        z_m[h].wait_recv()
        swap[5][h] = across(5, h)
        zr[h].wait_recv()
        swap[7][h] = across(7, h)
    for o in (5, 6, 7):
        swap[o][0].wait_recv()
        swap[o][1].wait_recv()

    ones = jnp.ones((128, 128), BF)

    def dense(b, carry):
        total = acc[b] + band(b, 5) + band(b, 6) + band(b, 7)
        deg = degs[b]
        agg = (total / (dot(deg, ones) + 1.0)).astype(BF)
        both = jnp.concatenate([f0[core, b], agg], axis=1)
        fa[b] = both
        v = dot(both, wcat[...]) + bias[...].astype(F32).reshape(1, 256)
        v2 = v * v
        th = jnp.tanh(GELU_A * (v + GELU_B * v * v2))
        up = 0.5 * (1.0 + th)
        lo[b] = (v * up).astype(BF)
        slope = up + 0.5 * v * (1.0 - th * th) * (GELU_A + (3.0 * GELU_A * GELU_B) * v2)
        g = (cotv[b].astype(F32) * slope).astype(BF)
        gp[b] = g
        back = dot(w_neigh[...], g, NT)
        sigt[b] = (back / (dot(ones, deg, NT) + 1.0)).astype(BF)
        return carry

    lax.fori_loop(0, 16, dense, 0, unroll=2)
    lo_c = pltpu.make_async_copy(lo, lo_out, ls.at[L_LO])
    lo_c.start()

    def product(n2, k):
        b = idx[k, n2]
        lanes = pl.ds(pl.multiple_of((n2 % 2) * 128, 128), 128)
        return dot(sigt[b], tileb[b, n2 // 2, :, lanes])

    def part(n2):
        total = product(n2, 0)
        runs[0] = total
        for k in range(1, 16):
            total = total * idx[16 + k, n2].astype(F32) + product(n2, k)
            runs[k] = total

    def run_of(n2, t):
        return runs[idx[32 + t, n2]] * idx[48 + t, n2].astype(F32)

    def chip_of(j):
        dx, dz = 0, 0
        for i, (ax, az) in enumerate(SEND):
            dx = dx + jnp.where(j == i, ax, 0)
            dz = dz + jnp.where(j == i, az, 0)
        return chip_at(dx, dz)

    def swap_part(j):
        return remote(sd2d.at[j], rd2d.at[j], S_PART + j, partner)

    def link(i, src, dst, dev):
        return remote(src, dst, S_RS + i, dev)

    leaf = [
        link(0, pbuf.at[0], rz, zz),
        link(1, pbuf.at[1], rxm, xp),
        link(2, pbuf.at[2], rxp, xm),
        link(3, pbuf.at[3, hi_h], rfm.at[hi_h], xp),
        link(4, pbuf.at[4, lo_h], rfp.at[lo_h], xm),
    ]

    def step(j, carry):
        @pl.when(j < 8)
        def _():
            n2 = chip_of(j) * 2 + (1 - core)
            part(n2)
            for t in range(16):
                sd2d[j, t] = run_of(n2, t).astype(BF)
            swap_part(j).start()

        @pl.when(j > 0)
        def _():
            i = j - 1
            n2 = chip_of(i) * 2 + core
            part(n2)
            swap_part(i).wait_recv()
            for t in range(16):
                pbuf[i, t] = (run_of(n2, t) + rd2d[i, t].astype(F32)).astype(BF)
            for q in range(3):

                @pl.when(i == q)
                def _(q=q):
                    leaf[q].start()

        return carry

    lax.fori_loop(0, 9, step, 0)
    pending.extend(leaf)

    push_c = [None] * WIDE
    for j in range(WIDE):
        there = (w + j) % WIDE
        sums = dot(sigt[rrow[0, there]], offb[there]).astype(BF)
        if j:
            pushs[j] = sums
            push_c[j] = send(pushs.at[j], pushr.at[WIDE - j], S_PUSH + j, far(j))
        else:
            pushr[0] = sums

    gsum_w = jnp.zeros((256, 256), F32)

    def weights(b, tot):
        return tot + dot(fa[b], gp[b], TN)

    def biases(b, tot):
        return tot + dot(jnp.ones((8, 128), BF), gp[b])

    grad_w = lax.fori_loop(0, 16, weights, gsum_w)
    grad_b = lax.fori_loop(0, 16, biases, jnp.zeros((8, 256), F32))
    for h in range(2):
        for p in range(8):
            gsrc[h, p, 0:16] = grad_w[h * 128 + p * 16 : h * 128 + p * 16 + 16]
            gsrc[h, p, 16:24] = grad_b
    g_pair = send(gsrc.at[1 - core], grx, S_GPAIR, partner)

    def base(b, carry):
        baset[b] = dot(w_self[...], gp[b], NT)
        return carry

    lax.fori_loop(0, 16, base, 0, unroll=2)

    g_pair.wait_recv()
    gsum[...] = gsrc[core] + grx[...]
    gw_c = [None] * WIDE
    for j in range(1, WIDE):
        gw_c[j] = send(gsum.at[(w + j) % WIDE], gwr.at[WIDE - j], S_GW + j, far(j))

    leaf[0].wait_recv()

    def add_one(t, carry):
        pbuf[5, t] = (pbuf[5, t].astype(F32) + rz[t].astype(F32)).astype(BF)
        return carry

    lax.fori_loop(0, 16, add_one, 0)
    half_a = send(pbuf.at[5, lo_h], rha, S_RS + 5, xp)
    half_b = send(pbuf.at[5, hi_h], rhb, S_RS + 6, xm)

    for j in range(1, WIDE):
        gw_c[j].wait_recv()
    tot = gsum[w]
    for j in range(1, WIDE):
        tot += gwr[j]
    gown[...] = tot
    gn_c = [None] * WIDE
    for o in range(1, 8):
        gn_c[o] = send(gown, gnr.at[chip], S_GN + o, near(*OFF[o]))

    leaf[3].start()
    leaf[4].start()

    leaf[1].wait_recv()
    leaf[2].wait_recv()

    def add_two(t, carry):
        both = rxp[t].astype(F32) + rxm[t].astype(F32)
        pbuf[6, t] = (pbuf[6, t].astype(F32) + both).astype(BF)
        return carry

    lax.fori_loop(0, 16, add_two, 0)
    last_z = send(pbuf.at[6], rfz, S_RS + 7, zz)

    for j in range(1, WIDE):
        push_c[j].wait_recv()

    def off_back(t, carry):
        total = baset[t] + pbuf[7, t].astype(F32)
        for j in range(WIDE):
            m = jnp.where(reqr[j][0:1, :] == t, 1.0, 0.0)
            total += pushr[j].astype(F32) * m
        baset[t] = total
        return carry

    lax.fori_loop(0, 16, off_back, 0)

    half_a.wait_recv()

    def add_a(t, carry):
        pbuf[3, t] = (pbuf[3, t].astype(F32) + rha[t].astype(F32)).astype(BF)
        return carry

    lax.fori_loop(0, 8, add_a, 0)
    last_p = send(pbuf.at[3, lo_h], rfm.at[lo_h], S_RS + 8, xp)
    half_b.wait_recv()

    def add_b(t, carry):
        pbuf[4, 8 + t] = (pbuf[4, 8 + t].astype(F32) + rhb[t].astype(F32)).astype(BF)
        return carry

    lax.fori_loop(0, 8, add_b, 0)
    last_m = send(pbuf.at[4, hi_h], rfp.at[hi_h], S_RS + 9, xm)

    for o in range(1, 8):
        gn_c[o].wait_recv()
    gnr[chip] = gown[...]
    tot = gnr[0]
    for c in range(1, 8):
        tot += gnr[c]
    gfin[w] = tot
    ga_c = [None] * WIDE
    for j in range(1, WIDE):
        ga_c[j] = send(gfin.at[w], gfin.at[w], S_GA + j, far(j))

    for j in range(1, WIDE):
        ga_c[j].wait_recv()
    gall[core] = gfin[...]
    g_last = send(gfin, gall.at[core], S_GB, partner)

    leaf[3].wait_recv()
    leaf[4].wait_recv()
    last_z.wait_recv()
    g_last.wait_recv()
    g_c = pltpu.make_async_copy(gall, g_out, ls.at[L_G])
    g_c.start()

    gf_c = []

    def finish(h):
        for i in range(8):
            t = 8 * h + i
            total = baset[t] + rfp[t].astype(F32) + rfm[t].astype(F32) + rfz[t].astype(F32)
            gfv[t] = total.T
            c = pltpu.make_async_copy(gfv.at[t], gf_out.at[t], ls.at[L_GF + t])
            c.start()
            gf_c.append(c)

    last_p.wait_recv()
    finish(0)
    last_m.wait_recv()
    finish(1)

    for c in gf_c:
        c.wait()
    lo_c.wait()
    g_c.wait()
    for c in pending:
        c.wait_send()

    def drain(j, carry):
        swap_part(j).wait_send()
        return carry

    lax.fori_loop(0, 8, drain, 0)


def settle(lo_in, gf_in, g_in, lo_out, gf_out, gs_out, gn_out, gb_out, lov, gfv, gv, ls):
    count = 4
    g_c = pltpu.make_async_copy(g_in, gv, ls.at[4 * count])
    g_c.start()
    loads = []
    stores = []
    for i in range(count):
        part = pl.ds(4 * i, 4)
        for k, (src, mid, dst) in enumerate(((lo_in, lov, lo_out), (gf_in, gfv, gf_out))):
            n = 2 * i + k
            loads.append(pltpu.make_async_copy(src.at[part], mid.at[part], ls.at[n]))
            stores.append(
                pltpu.make_async_copy(mid.at[part], dst.at[part], ls.at[2 * count + n])
            )
            loads[-1].start()
    for load, store in zip(loads, stores):
        load.wait()
        store.start()
    g_c.wait()
    factor = 262144 ** (-0.5)
    for p in range(8):
        gs_out[p * 16 : p * 16 + 16] = gv[0, p, 0:16] * factor
        gn_out[p * 16 : p * 16 + 16] = gv[1, p, 0:16] * factor
    gb_out[...] = gv[0, 0, 16:17] * factor
    for store in stores:
        store.wait()


def shards(
    features, band_tiles, band_cols, off_tiles, req_block, req_row, req_valid,
    weight_self, weight_neigh, bias_term, cotangent,
):
    hbm = pl.BlockSpec(memory_space=pl.ANY)
    vmem = pl.BlockSpec(memory_space=pltpu.VMEM)
    smem = pl.BlockSpec(memory_space=pltpu.SMEM)
    block = (16, 128, 128)
    v = pltpu.VMEM
    scratch = [v((2,) + block, BF) for _ in range(8)]
    scratch += [
        v((16, 8, 128, 256), BF),
        v((3,) + block, I32),
        v((8, 128, 128), I32),
        v((8, 128, 128), BF),
        v((16, 128, 256), BF),
        v(block, F32),
        v(block, BF),
        v((16, 128, 256), BF),
        v((16, 128, 256), BF),
        v((16, 128, 256), BF),
        v(block, BF),
        v(block, F32),
        v((256, 256), BF),
        v((8,) + block, BF),
        v((8,) + block, BF),
        v((8,) + block, BF),
        v(block, BF),
        v(block, BF),
        v(block, BF),
        v((8, 128, 128), BF),
        v((8, 128, 128), BF),
        v(block, BF),
        v(block, BF),
        v(block, BF),
        v(block, F32),
        v(block, F32),
        v((64, 128), I32),
        pltpu.SMEM((64, 128), I32),
        v((8, 8, 128), I32),
        v((8, 8, 128), I32),
        v((8, 128, 128), BF),
        v((8, 128, 128), BF),
        v((8, 128, 128), F32),
        v((8, 128, 128), BF),
        v((8, 128, 128), BF),
        v((2, 8, 24, 256), F32),
        v((8, 24, 256), F32),
        v((8, 24, 256), F32),
        v((8, 24, 256), F32),
        v((24, 256), F32),
        v((8, 24, 256), F32),
        v((8, 24, 256), F32),
        v((2, 8, 24, 256), F32),
        pltpu.SemaphoreType.DMA((S_COUNT,)),
        pltpu.SemaphoreType.DMA((S_COUNT,)),
        pltpu.SemaphoreType.DMA((L_COUNT,)),
    ]
    layer_out, grad_feat, grads = pl.pallas_call(
        body,
        out_shape=(
            jax.ShapeDtypeStruct((16, 128, 256), BF),
            jax.ShapeDtypeStruct(block, F32),
            jax.ShapeDtypeStruct((2, 8, 24, 256), F32),
        ),
        in_specs=[hbm, hbm, smem, vmem, hbm, smem, smem, smem, vmem, vmem, vmem, hbm],
        out_specs=(hbm, hbm, hbm),
        scratch_shapes=scratch,
        compiler_params=pltpu.CompilerParams(
            collective_id=0, has_side_effects=True, vmem_limit_bytes=60 * 1024 * 1024
        ),
        name="sage",
    )(
        features.reshape(block), band_tiles, band_cols, band_cols, off_tiles[0],
        req_block, req_row, req_valid, weight_self, weight_neigh,
        bias_term, cotangent.reshape(16, 128, 256),
    )
    layer_out, grad_feat, grad_self, grad_neigh, grad_bias = pl.pallas_call(
        settle,
        out_shape=(
            jax.ShapeDtypeStruct((16, 128, 256), BF),
            jax.ShapeDtypeStruct(block, F32),
            jax.ShapeDtypeStruct((128, 256), F32),
            jax.ShapeDtypeStruct((128, 256), F32),
            jax.ShapeDtypeStruct((1, 256), F32),
        ),
        in_specs=[hbm, hbm, hbm],
        out_specs=(hbm, hbm, vmem, vmem, vmem),
        scratch_shapes=[
            v((16, 128, 256), BF),
            v(block, F32),
            v((2, 8, 24, 256), F32),
            pltpu.SemaphoreType.DMA((17,)),
        ],
        name="settle",
    )(layer_out, grad_feat, grads)
    return (
        layer_out.reshape(2048, 256),
        grad_feat.reshape(2048, 128),
        grad_self,
        grad_neigh,
        grad_bias.reshape(256),
    )


def solution(mesh):
    placed = (
        P(("wide", "narrow"), None),
        P(("wide", "narrow"), None, None, None),
        P(("wide", "narrow"), None),
        P(("wide", "narrow"), None, None, None),
        P(("wide", "narrow"), None),
        P(("wide", "narrow"), None),
        P(("wide", "narrow"), None),
        P(),
        P(),
        P(),
        P(("wide", "narrow"), None),
    )
    return jax.shard_map(
        shards,
        mesh=mesh,
        in_specs=placed,
        out_specs=(P(("wide", "narrow"), None), P(("wide", "narrow"), None), P(), P(), P()),
        check_vma=False,
    )
```

```python
import jax
import jax.numpy as jnp
from jax import lax
from jax.experimental import pallas as pl
from jax.experimental.pallas import tpu as pltpu
from jax.sharding import PartitionSpec as P

BF = jnp.bfloat16
F32 = jnp.float32
I32 = jnp.int32
MESH = pl.DeviceIdType.MESH
NT = (((1,), (1,)), ((), ()))
TN = (((0,), (0,)), ((), ()))

OFF = ((0, 0), (1, 0), (3, 0), (0, 1), (2, 0), (1, 1), (3, 1), (2, 1))
SEND = ((2, 1), (1, 1), (3, 1), (1, 0), (3, 0), (2, 0), (0, 1), (0, 0))
WIDE = 8
GELU_A = 0.7978845608
GELU_B = 0.044715

S_OWN, S_RELAY, S_PAIR, S_REQ, S_FET, S_PUSH = 0, 8, 16, 32, 40, 48
S_GPAIR, S_GW, S_GN, S_GA, S_GB, S_PART, S_RS, S_COUNT = 56, 57, 65, 73, 81, 82, 90, 104
L_TILE, L_FEAT, L_OFF, L_COT, L_IDX, L_LO, L_GF, L_G, L_REQ, L_COUNT = 0, 3, 4, 5, 6, 7, 8, 24, 25, 26


def dot(a, b, dims=None):
    if dims is None:
        return jnp.dot(a, b, preferred_element_type=F32)
    return lax.dot_general(a, b, dims, preferred_element_type=F32)


def body(
    feat, tiles, cols, cols_v, offs, rblock, rrow, rvalid, w_self, w_neigh, bias, cot,
    lo_out, gf_out, g_out,
    f0, f1, f2, f3, f4, f5, f6, f7,
    tileb, stage, offi, offb, cotv, acc, degs, fa, gp, lo, sigt, runs, wcat,
    sd2d, rd2d, pbuf, rz, rxp, rxm, rha, rhb, rfp, rfm, rfz, baset, gfv,
    idx_v, idx, reqs, reqr, asked, sel, fetr, pull, pushs, pushr,
    gsrc, grx, gsum, gwr, gown, gnr, gfin, gall,
    ss, rs, ls,
):
    fs = (f0, f1, f2, f3, f4, f5, f6, f7)
    me = lax.axis_index("narrow")
    w = lax.axis_index("wide")
    core = me % 2
    chip = me // 2
    x = chip % 4
    z = chip // 4

    def chip_at(dx, dz):
        return ((z + dz) % 2) * 4 + (x + dx) % 4

    def near(dx, dz):
        return (w, chip_at(dx, dz) * 2 + core)

    partner = (w, chip * 2 + (1 - core))
    xp, xm, zz = near(1, 0), near(3, 0), near(0, 1)

    def far(j):
        return ((w + j) % WIDE, me)

    pending = []

    def remote(src, dst, i, dev):
        return pltpu.make_async_remote_copy(
            src_ref=src, dst_ref=dst, send_sem=ss.at[i], recv_sem=rs.at[i],
            device_id=dev, device_id_type=MESH,
        )

    def send(src, dst, i, dev):
        c = remote(src, dst, i, dev)
        c.start()
        pending.append(c)
        return c

    def load_tiles(b, slot):
        return pltpu.make_async_copy(tiles.at[b], stage.at[slot], ls.at[L_TILE + slot])

    own = pltpu.make_async_copy(feat, f0.at[core], ls.at[L_FEAT])
    own.start()
    off_load = pltpu.make_async_copy(offs, offi, ls.at[L_OFF])
    off_load.start()
    load_tiles(0, 0).start()
    load_tiles(1, 1).start()
    cot_load = pltpu.make_async_copy(cot, cotv, ls.at[L_COT])
    cot_load.start()

    bar = pltpu.get_barrier_semaphore()
    pl.semaphore_signal(bar, inc=1, device_id=partner, device_id_type=MESH)
    for dx, dz in OFF[1:]:
        pl.semaphore_signal(bar, inc=1, device_id=near(dx, dz), device_id_type=MESH)
    for j in range(1, WIDE):
        pl.semaphore_signal(bar, inc=1, device_id=far(j), device_id_type=MESH)
    for b in range(WIDE):
        reqs[b] = jnp.full((8, 128), rblock[0, b], I32)
    pl.semaphore_wait(bar, 15)

    lo_h, hi_h = pl.ds(0, 8), pl.ds(8, 8)
    halves = (lo_h, hi_h)
    to_p = [None, None]
    to_m = [None, None]
    to_z = [None, None]
    req_c = [None] * WIDE
    for j in range(1, WIDE):
        req_c[j] = send(reqs.at[(w + j) % WIDE], reqr.at[WIDE - j], S_REQ + j, far(j))
    to_p[0] = send(feat.at[lo_h], f2.at[core, lo_h], S_OWN + 0, xp)
    to_m[1] = send(feat.at[hi_h], f1.at[core, hi_h], S_OWN + 1, xm)
    to_z[0] = send(feat.at[lo_h], f3.at[core, lo_h], S_OWN + 2, zz)
    to_p[1] = send(feat.at[hi_h], f2.at[core, hi_h], S_OWN + 3, xp)
    to_m[0] = send(feat.at[lo_h], f1.at[core, lo_h], S_OWN + 4, xm)
    to_z[1] = send(feat.at[hi_h], f3.at[core, hi_h], S_OWN + 5, zz)
    pair0 = send(feat, f0.at[core], S_PAIR, partner)

    c16 = cols_v[...]
    ib = lax.broadcasted_iota(I32, (16, 16), 0)
    rank = jnp.zeros((16, 16), I32)
    prev = jnp.zeros((16, 16), I32)
    count = jnp.zeros((16, 16), I32)
    upto = jnp.zeros((16, 16), I32)
    for b in range(16):
        row = jnp.broadcast_to(c16[b : b + 1, :], (16, 16))
        same = row == c16
        before = same & (ib > b)
        rank += jnp.where((row < c16) | before, 1, 0)
        prev += jnp.where(before, 1, 0)
        count += jnp.where(row == ib, 1, 0)
        upto += jnp.where(row <= ib, 1, 0)
    order = jnp.zeros((16, 16), I32)
    keep = jnp.zeros((16, 16), I32)
    for b in range(16):
        hit = jnp.broadcast_to(rank[b : b + 1, :], (16, 16)) == ib
        order += jnp.where(hit, b, 0)
        keep += jnp.where(hit & (jnp.broadcast_to(prev[b : b + 1, :], (16, 16)) > 0), 1, 0)
    idx_v[...] = jnp.zeros((64, 128), I32)
    idx_v[0:16, 0:16] = order
    idx_v[16:32, 0:16] = keep
    idx_v[32:48, 0:16] = jnp.maximum(upto - 1, 0)
    idx_v[48:64, 0:16] = jnp.where(count > 0, 1, 0)
    idx_load = pltpu.make_async_copy(idx_v, idx, ls.at[L_IDX])
    idx_load.start()
    wcat[0:128, :] = w_self[...]
    wcat[128:256, :] = w_neigh[...]

    own.wait()
    off_load.wait()

    def convert(b, carry):
        slot = b % 3
        load_tiles(b, slot).wait()

        @pl.when(b + 2 < 16)
        def _():
            load_tiles(b + 2, (b + 2) % 3).start()

        total = jnp.zeros((128, 128), I32)
        for c in range(8):
            lft = stage[slot, 2 * c]
            rgt = stage[slot, 2 * c + 1]
            total += lft + rgt
            tileb[b, c] = jnp.concatenate([lft, rgt], axis=1).astype(F32).astype(BF)
        for j in range(WIDE):
            use = jnp.where(rrow[0, j] == b, rvalid[0, j], 0)
            total += offi[j] * use
        degs[b] = total.astype(F32).astype(BF)
        return carry

    lax.fori_loop(0, 6, convert, 0)

    reqr[0] = reqs[w]
    for j in range(WIDE):
        offb[j] = (offi[j] * rvalid[0, j]).astype(BF)
    fet_c = [None] * WIDE
    for j in range(1, WIDE):
        req_c[j].wait_recv()
    ask_load = pltpu.make_async_copy(reqr, asked, ls.at[L_REQ])
    ask_load.start()
    pair0.wait_recv()
    ask_load.wait()
    for j in range(1, WIDE):
        sel[j] = f0[core, asked[WIDE - j, 0, 0]]
        fet_c[j] = send(sel.at[j], fetr.at[j], S_FET + j, far(WIDE - j))

    def band(b, o):
        c = chip_at(*OFF[o])
        rhs = jnp.concatenate(
            [fs[o][0, cols[b, 2 * c]], fs[o][1, cols[b, 2 * c + 1]]], axis=0
        )
        return dot(tileb[b, c], rhs)

    def across(o, h):
        return send(fs[o].at[core, halves[h]], fs[o].at[core, halves[h]], S_PAIR + 2 * o + h, partner)

    swap = [[None, None] for _ in OFF]
    to_p[0].wait_recv()
    rel_p = send(f2.at[core, lo_h], f4.at[core, lo_h], S_RELAY + 0, xp)
    to_m[1].wait_recv()
    rel_m = send(f1.at[core, hi_h], f4.at[core, hi_h], S_RELAY + 1, xm)
    swap[2][0] = across(2, 0)
    swap[1][1] = across(1, 1)
    to_z[0].wait_recv()
    z_p = [None, None]
    z_m = [None, None]
    z_p[0] = send(f3.at[core, lo_h], f6.at[core, lo_h], S_RELAY + 2, xp)
    z_m[0] = send(f3.at[core, lo_h], f5.at[core, lo_h], S_RELAY + 3, xm)
    swap[3][0] = across(3, 0)

    lax.fori_loop(6, 16, convert, 0)

    def first(b, carry):
        acc[b] = band(b, 0)
        return carry

    lax.fori_loop(0, 16, first, 0, unroll=2)

    to_z[1].wait_recv()
    z_p[1] = send(f3.at[core, hi_h], f6.at[core, hi_h], S_RELAY + 4, xp)
    z_m[1] = send(f3.at[core, hi_h], f5.at[core, hi_h], S_RELAY + 5, xm)
    swap[3][1] = across(3, 1)
    to_p[1].wait_recv()
    swap[2][1] = across(2, 1)
    to_m[0].wait_recv()
    swap[1][0] = across(1, 0)

    for o in (1, 2, 3):
        swap[o][0].wait_recv()
        swap[o][1].wait_recv()

    def second(b, carry):
        total = acc[b] + band(b, 1) + band(b, 2) + band(b, 3)
        acc[b] = total
        return carry

    lax.fori_loop(0, 16, second, 0, unroll=2)

    rel_p.wait_recv()
    zr = [None, None]
    zr[0] = send(f4.at[core, lo_h], f7.at[core, lo_h], S_RELAY + 6, zz)
    swap[4][0] = across(4, 0)
    rel_m.wait_recv()
    zr[1] = send(f4.at[core, hi_h], f7.at[core, hi_h], S_RELAY + 7, zz)
    swap[4][1] = across(4, 1)
    for j in range(1, WIDE):
        fet_c[j].wait_recv()
    fetr[0] = f0[core, rblock[0, w]]
    for j in range(WIDE):
        pull[j] = dot(offb[(w + j) % WIDE], fetr[j])

    swap[4][0].wait_recv()
    swap[4][1].wait_recv()

    def third(b, carry):
        total = acc[b] + band(b, 4)
        for j in range(WIDE):
            use = jnp.where(rrow[0, (w + j) % WIDE] == b, 1, 0).astype(F32)
            total += pull[j] * use
        acc[b] = total
        return carry

    lax.fori_loop(0, 16, third, 0, unroll=2)
    idx_load.wait()
    cot_load.wait()

    for h in range(2):
        z_p[h].wait_recv()
        swap[6][h] = across(6, h)
        z_m[h].wait_recv()
        swap[5][h] = across(5, h)
        zr[h].wait_recv()
        swap[7][h] = across(7, h)
    for o in (5, 6, 7):
        swap[o][0].wait_recv()
        swap[o][1].wait_recv()

    ones = jnp.ones((128, 128), BF)

    def dense(b, carry):
        total = acc[b] + band(b, 5) + band(b, 6) + band(b, 7)
        deg = degs[b]
        agg = (total / (dot(deg, ones) + 1.0)).astype(BF)
        both = jnp.concatenate([f0[core, b], agg], axis=1)
        fa[b] = both
        v = dot(both, wcat[...]) + bias[...].astype(F32).reshape(1, 256)
        v2 = v * v
        th = jnp.tanh(GELU_A * (v + GELU_B * v * v2))
        up = 0.5 * (1.0 + th)
        lo[b] = (v * up).astype(BF)
        slope = up + 0.5 * v * (1.0 - th * th) * (GELU_A + (3.0 * GELU_A * GELU_B) * v2)
        g = (cotv[b].astype(F32) * slope).astype(BF)
        gp[b] = g
        back = dot(w_neigh[...], g, NT)
        sigt[b] = (back / (dot(ones, deg, NT) + 1.0)).astype(BF)
        return carry

    lax.fori_loop(0, 16, dense, 0, unroll=2)
    lo_c = pltpu.make_async_copy(lo, lo_out, ls.at[L_LO])
    lo_c.start()

    def product(n2, k):
        b = idx[k, n2]
        lanes = pl.ds(pl.multiple_of((n2 % 2) * 128, 128), 128)
        return dot(sigt[b], tileb[b, n2 // 2, :, lanes])

    def part(n2):
        total = product(n2, 0)
        runs[0] = total
        for k in range(1, 16):
            total = total * idx[16 + k, n2].astype(F32) + product(n2, k)
            runs[k] = total

    def run_of(n2, t):
        return runs[idx[32 + t, n2]] * idx[48 + t, n2].astype(F32)

    def chip_of(j):
        dx, dz = 0, 0
        for i, (ax, az) in enumerate(SEND):
            dx = dx + jnp.where(j == i, ax, 0)
            dz = dz + jnp.where(j == i, az, 0)
        return chip_at(dx, dz)

    def swap_part(j):
        return remote(sd2d.at[j], rd2d.at[j], S_PART + j, partner)

    def link(i, src, dst, dev):
        return remote(src, dst, S_RS + i, dev)

    leaf = [
        link(0, pbuf.at[0], rz, zz),
        link(1, pbuf.at[1], rxm, xp),
        link(2, pbuf.at[2], rxp, xm),
        link(3, pbuf.at[3, hi_h], rfm.at[hi_h], xp),
        link(4, pbuf.at[4, lo_h], rfp.at[lo_h], xm),
    ]

    def step(j, carry):
        @pl.when(j < 8)
        def _():
            n2 = chip_of(j) * 2 + (1 - core)
            part(n2)
            for t in range(16):
                sd2d[j, t] = run_of(n2, t).astype(BF)
            swap_part(j).start()

        @pl.when(j > 0)
        def _():
            i = j - 1
            n2 = chip_of(i) * 2 + core
            part(n2)
            swap_part(i).wait_recv()
            for t in range(16):
                pbuf[i, t] = (run_of(n2, t) + rd2d[i, t].astype(F32)).astype(BF)
            for q in range(3):

                @pl.when(i == q)
                def _(q=q):
                    leaf[q].start()

        return carry

    lax.fori_loop(0, 9, step, 0)
    pending.extend(leaf)

    push_c = [None] * WIDE
    for j in range(WIDE):
        there = (w + j) % WIDE
        sums = dot(sigt[rrow[0, there]], offb[there]).astype(BF)
        if j:
            pushs[j] = sums
            push_c[j] = send(pushs.at[j], pushr.at[WIDE - j], S_PUSH + j, far(j))
        else:
            pushr[0] = sums

    gsum_w = jnp.zeros((256, 256), F32)

    def weights(b, tot):
        return tot + dot(fa[b], gp[b], TN)

    def biases(b, tot):
        return tot + dot(jnp.ones((8, 128), BF), gp[b])

    grad_w = lax.fori_loop(0, 16, weights, gsum_w)
    grad_b = lax.fori_loop(0, 16, biases, jnp.zeros((8, 256), F32))
    for h in range(2):
        for p in range(8):
            gsrc[h, p, 0:16] = grad_w[h * 128 + p * 16 : h * 128 + p * 16 + 16]
            gsrc[h, p, 16:24] = grad_b
    g_pair = send(gsrc.at[1 - core], grx, S_GPAIR, partner)

    def base(b, carry):
        baset[b] = dot(w_self[...], gp[b], NT)
        return carry

    lax.fori_loop(0, 16, base, 0, unroll=2)

    g_pair.wait_recv()
    gsum[...] = gsrc[core] + grx[...]
    gw_c = [None] * WIDE
    for j in range(1, WIDE):
        gw_c[j] = send(gsum.at[(w + j) % WIDE], gwr.at[WIDE - j], S_GW + j, far(j))

    leaf[0].wait_recv()

    def add_one(t, carry):
        pbuf[5, t] = (pbuf[5, t].astype(F32) + rz[t].astype(F32)).astype(BF)
        return carry

    lax.fori_loop(0, 16, add_one, 0)
    half_a = send(pbuf.at[5, lo_h], rha, S_RS + 5, xp)
    half_b = send(pbuf.at[5, hi_h], rhb, S_RS + 6, xm)

    for j in range(1, WIDE):
        gw_c[j].wait_recv()
    tot = gsum[w]
    for j in range(1, WIDE):
        tot += gwr[j]
    gown[...] = tot
    gn_c = [None] * WIDE
    for o in range(1, 8):
        gn_c[o] = send(gown, gnr.at[chip], S_GN + o, near(*OFF[o]))

    leaf[3].start()
    leaf[4].start()

    leaf[1].wait_recv()
    leaf[2].wait_recv()

    def add_two(t, carry):
        both = rxp[t].astype(F32) + rxm[t].astype(F32)
        pbuf[6, t] = (pbuf[6, t].astype(F32) + both).astype(BF)
        return carry

    lax.fori_loop(0, 16, add_two, 0)
    last_z = send(pbuf.at[6], rfz, S_RS + 7, zz)

    for j in range(1, WIDE):
        push_c[j].wait_recv()

    def off_back(t, carry):
        total = baset[t] + pbuf[7, t].astype(F32)
        for j in range(WIDE):
            m = jnp.where(reqr[j][0:1, :] == t, 1.0, 0.0)
            total += pushr[j].astype(F32) * m
        baset[t] = total
        return carry

    lax.fori_loop(0, 16, off_back, 0)

    half_a.wait_recv()

    def add_a(t, carry):
        pbuf[3, t] = (pbuf[3, t].astype(F32) + rha[t].astype(F32)).astype(BF)
        return carry

    lax.fori_loop(0, 8, add_a, 0)
    last_p = send(pbuf.at[3, lo_h], rfm.at[lo_h], S_RS + 8, xp)
    half_b.wait_recv()

    def add_b(t, carry):
        pbuf[4, 8 + t] = (pbuf[4, 8 + t].astype(F32) + rhb[t].astype(F32)).astype(BF)
        return carry

    lax.fori_loop(0, 8, add_b, 0)
    last_m = send(pbuf.at[4, hi_h], rfp.at[hi_h], S_RS + 9, xm)

    for o in range(1, 8):
        gn_c[o].wait_recv()
    gnr[chip] = gown[...]
    tot = gnr[0]
    for c in range(1, 8):
        tot += gnr[c]
    gfin[w] = tot
    ga_c = [None] * WIDE
    for j in range(1, WIDE):
        ga_c[j] = send(gfin.at[w], gfin.at[w], S_GA + j, far(j))

    for j in range(1, WIDE):
        ga_c[j].wait_recv()
    gall[core] = gfin[...]
    g_last = send(gfin, gall.at[core], S_GB, partner)

    leaf[3].wait_recv()
    leaf[4].wait_recv()
    last_z.wait_recv()
    g_last.wait_recv()
    g_c = pltpu.make_async_copy(gall, g_out, ls.at[L_G])
    g_c.start()

    gf_c = []

    def finish(h):
        for i in range(8):
            t = 8 * h + i
            total = baset[t] + rfp[t].astype(F32) + rfm[t].astype(F32) + rfz[t].astype(F32)
            gfv[t] = total.T
            c = pltpu.make_async_copy(gfv.at[t], gf_out.at[t], ls.at[L_GF + t])
            c.start()
            gf_c.append(c)

    last_p.wait_recv()
    finish(0)
    last_m.wait_recv()
    finish(1)

    for c in gf_c:
        c.wait()
    lo_c.wait()
    g_c.wait()
    for c in pending:
        c.wait_send()

    def drain(j, carry):
        swap_part(j).wait_send()
        return carry

    lax.fori_loop(0, 8, drain, 0)


def settle(lo_in, gf_in, g_in, lo_out, gf_out, gs_out, gn_out, gb_out, lov, gfv, gv, ls):
    count = 4
    g_c = pltpu.make_async_copy(g_in, gv, ls.at[4 * count])
    g_c.start()
    loads = []
    stores = []
    for i in range(count):
        part = pl.ds(4 * i, 4)
        for k, (src, mid, dst) in enumerate(((lo_in, lov, lo_out), (gf_in, gfv, gf_out))):
            n = 2 * i + k
            loads.append(pltpu.make_async_copy(src.at[part], mid.at[part], ls.at[n]))
            stores.append(
                pltpu.make_async_copy(mid.at[part], dst.at[part], ls.at[2 * count + n])
            )
            loads[-1].start()
    for load, store in zip(loads, stores):
        load.wait()
        store.start()
    g_c.wait()
    factor = 262144 ** (-0.5)
    for p in range(8):
        gs_out[p * 16 : p * 16 + 16] = gv[0, p, 0:16] * factor
        gn_out[p * 16 : p * 16 + 16] = gv[1, p, 0:16] * factor
    gb_out[...] = gv[0, 0, 16:17] * factor
    for store in stores:
        store.wait()


def shards(
    features, band_tiles, band_cols, off_tiles, req_block, req_row, req_valid,
    weight_self, weight_neigh, bias_term, cotangent,
):
    hbm = pl.BlockSpec(memory_space=pl.ANY)
    vmem = pl.BlockSpec(memory_space=pltpu.VMEM)
    smem = pl.BlockSpec(memory_space=pltpu.SMEM)
    block = (16, 128, 128)
    v = pltpu.VMEM
    scratch = [v((2,) + block, BF) for _ in range(8)]
    scratch += [
        v((16, 8, 128, 256), BF),
        v((3,) + block, I32),
        v((8, 128, 128), I32),
        v((8, 128, 128), BF),
        v((16, 128, 256), BF),
        v(block, F32),
        v(block, BF),
        v((16, 128, 256), BF),
        v((16, 128, 256), BF),
        v((16, 128, 256), BF),
        v(block, BF),
        v(block, F32),
        v((256, 256), BF),
        v((8,) + block, BF),
        v((8,) + block, BF),
        v((8,) + block, BF),
        v(block, BF),
        v(block, BF),
        v(block, BF),
        v((8, 128, 128), BF),
        v((8, 128, 128), BF),
        v(block, BF),
        v(block, BF),
        v(block, BF),
        v(block, F32),
        v(block, F32),
        v((64, 128), I32),
        pltpu.SMEM((64, 128), I32),
        v((8, 8, 128), I32),
        v((8, 8, 128), I32),
        pltpu.SMEM((8, 8, 128), I32),
        v((8, 128, 128), BF),
        v((8, 128, 128), BF),
        v((8, 128, 128), F32),
        v((8, 128, 128), BF),
        v((8, 128, 128), BF),
        v((2, 8, 24, 256), F32),
        v((8, 24, 256), F32),
        v((8, 24, 256), F32),
        v((8, 24, 256), F32),
        v((24, 256), F32),
        v((8, 24, 256), F32),
        v((8, 24, 256), F32),
        v((2, 8, 24, 256), F32),
        pltpu.SemaphoreType.DMA((S_COUNT,)),
        pltpu.SemaphoreType.DMA((S_COUNT,)),
        pltpu.SemaphoreType.DMA((L_COUNT,)),
    ]
    layer_out, grad_feat, grads = pl.pallas_call(
        body,
        out_shape=(
            jax.ShapeDtypeStruct((16, 128, 256), BF),
            jax.ShapeDtypeStruct(block, F32),
            jax.ShapeDtypeStruct((2, 8, 24, 256), F32),
        ),
        in_specs=[hbm, hbm, smem, vmem, hbm, smem, smem, smem, vmem, vmem, vmem, hbm],
        out_specs=(hbm, hbm, hbm),
        scratch_shapes=scratch,
        compiler_params=pltpu.CompilerParams(
            collective_id=0, has_side_effects=True, vmem_limit_bytes=60 * 1024 * 1024
        ),
        name="sage",
    )(
        features.reshape(block), band_tiles, band_cols, band_cols, off_tiles[0],
        req_block, req_row, req_valid, weight_self, weight_neigh,
        bias_term, cotangent.reshape(16, 128, 256),
    )
    layer_out, grad_feat, grad_self, grad_neigh, grad_bias = pl.pallas_call(
        settle,
        out_shape=(
            jax.ShapeDtypeStruct((16, 128, 256), BF),
            jax.ShapeDtypeStruct(block, F32),
            jax.ShapeDtypeStruct((128, 256), F32),
            jax.ShapeDtypeStruct((128, 256), F32),
            jax.ShapeDtypeStruct((1, 256), F32),
        ),
        in_specs=[hbm, hbm, hbm],
        out_specs=(hbm, hbm, vmem, vmem, vmem),
        scratch_shapes=[
            v((16, 128, 256), BF),
            v(block, F32),
            v((2, 8, 24, 256), F32),
            pltpu.SemaphoreType.DMA((17,)),
        ],
        name="settle",
    )(layer_out, grad_feat, grads)
    return (
        layer_out.reshape(2048, 256),
        grad_feat.reshape(2048, 128),
        grad_self,
        grad_neigh,
        grad_bias.reshape(256),
    )


def solution(mesh):
    placed = (
        P(("wide", "narrow"), None),
        P(("wide", "narrow"), None, None, None),
        P(("wide", "narrow"), None),
        P(("wide", "narrow"), None, None, None),
        P(("wide", "narrow"), None),
        P(("wide", "narrow"), None),
        P(("wide", "narrow"), None),
        P(),
        P(),
        P(),
        P(("wide", "narrow"), None),
    )
    return jax.shard_map(
        shards,
        mesh=mesh,
        in_specs=placed,
        out_specs=(P(("wide", "narrow"), None), P(("wide", "narrow"), None), P(), P(), P()),
        check_vma=False,
    )
```
